256 devices in a mesh: row: 16 (over z, core), col: 16 (over x, y).
Axes of the slice: x: 4, y: 4, z: 8, core: 2. Of those that a mesh axis runs over, the one named last changes fastest.
Arguments:
- matrix: bfloat16 [7, 4096, 7, 4096], P(None, 'row', None, 'col'), may hold values from -1 to 3
- pivots: int32 [2, 256], replicated, may hold values from 256 to 28671, as said below
Outputs:
- factored: bfloat16 [7, 4096, 7, 4096], P(None, 'row', None, 'col')
The draws below stay inside these ranges and needn't reach their ends.
Inputs may be any that keep to these rules, and one draw needn't show every extreme that they name: Within a step s the pivots[s, :] are distinct and lie in (s + 1) * 256 to 28671.
All inputs are finite; a program needn't handle non-finite values.
Results may differ from the reference program's by a relative error of at most 0.0059.
Values may be sent and summed in bfloat16 or wider, within the bound.
A program may use at most 64 MiB of HBM per device.

```python
import math
import jax
import jax.numpy as jnp
from jax import lax

NB = 256
STEPS = 2
NEWTON = 3
ORDER = 28672
ROW_CYCLES = 7
COL_CYCLES = 7
N_ROW = 16
N_COL = 16


def pivot_table(key):
    tables = []
    for panel_step in range(STEPS):
        key_pick = jax.random.fold_in(key, 101 + panel_step)
        key_order = jax.random.fold_in(key, 211 + panel_step)
        lowest = (panel_step + 1) * NB
        interior = jax.random.permutation(key_pick, ORDER - lowest - 2)[:NB - 2].astype(jnp.int32) + lowest + 1
        values = jnp.concatenate([jnp.array([lowest, ORDER - 1], dtype=jnp.int32), interior])
        shuffle = jax.random.permutation(key_order, NB)
        tables.append(values[shuffle])
    return jnp.stack(tables).astype(jnp.int32)


def draw_pivots(key, part):
    return pivot_table(key)


def draw_matrix(key, part):
    table = pivot_table(key)
    anchor = jnp.arange(ORDER, dtype=jnp.int32)
    sources = []
    for panel_step in range(STEPS):
        upper_rows = panel_step * NB + jnp.arange(NB, dtype=jnp.int32)
        chosen = table[panel_step]
        from_rows = anchor[chosen]
        moved_up = anchor[upper_rows]
        sources.append(from_rows)
        anchor = anchor.at[upper_rows].set(from_rows).at[chosen].set(moved_up)
    source_rows = jnp.concatenate(sources)
    panel_width = STEPS * NB
    key_base = jax.random.fold_in(key, 7)
    key_small = jax.random.fold_in(key, 11)
    key_diag = jax.random.fold_in(key, 17)
    noise_vals = jax.random.uniform(key_base, (ORDER, ORDER), jnp.float32, -1.0, 1.0)
    entries = noise_vals
    diag_vals = jnp.exp(jax.random.uniform(key_diag, (panel_width,), jnp.float32, math.log(1.2), math.log(3.0)))
    column = jnp.arange(ORDER, dtype=jnp.int32)[None, :]
    entries = jnp.where(column < panel_width, 0.4 * entries, entries)
    small_block = jax.random.uniform(key_small, (panel_width, panel_width), jnp.float32, -1.0 / NB, 1.0 / NB)
    entries = entries.at[source_rows, :panel_width].set(small_block)
    entries = entries.at[source_rows, jnp.arange(panel_width, dtype=jnp.int32)].set(diag_vals)
    return entries.astype(jnp.bfloat16).reshape(ROW_CYCLES, ORDER // ROW_CYCLES, COL_CYCLES, ORDER // COL_CYCLES)


def setup_inputs(seed: int = 0) -> dict:
    keys = jax.random.split(jax.random.key(seed), 3)
    matrix = draw_matrix(jax.random.fold_in(keys[2], 71), 0)
    pivots = draw_pivots(jax.random.fold_in(keys[2], 71), 0)
    return dict(matrix=matrix, pivots=pivots)


def newton_inverse(diag_block):
    identity = jnp.eye(diag_block.shape[0], dtype=jnp.float32)
    approx = identity / 3.0
    for _ in range(NEWTON):
        product = jnp.dot(diag_block, approx, precision=lax.Precision.HIGHEST)
        approx = jnp.dot(approx, 2.0 * identity - product, precision=lax.Precision.HIGHEST)
    return approx


def reference(matrix, pivots):
    current = matrix.reshape(ORDER, ORDER)
    all_rows = jnp.arange(ORDER, dtype=jnp.int32)
    for panel_step in range(STEPS):
        first_row = panel_step * NB
        after_row = first_row + NB
        chosen = pivots[panel_step].astype(jnp.int32)
        top_rows = current[first_row:after_row]
        picked = current[chosen]
        current = current.at[first_row:after_row].set(picked).at[chosen].set(top_rows)
        diag_block = current[first_row:after_row, first_row:after_row].astype(jnp.float32)
        inverse = newton_inverse(diag_block)
        below_mask = (all_rows >= after_row)[:, None]
        panel_vals = current[:, first_row:after_row].astype(jnp.float32)
        lower_panel = jnp.where(below_mask, jnp.dot(panel_vals, inverse, precision=lax.Precision.HIGHEST), 0.0).astype(jnp.bfloat16)
        right_mask = (all_rows >= after_row)[None, :]
        upper_rows = jnp.where(right_mask, current[first_row:after_row], jnp.zeros_like(current[first_row:after_row]))

        def update_rows(operands):
            block_vals, lower_block = operands
            change = jnp.dot(lower_block, upper_rows, preferred_element_type=jnp.float32)
            return (block_vals.astype(jnp.float32) - change).astype(jnp.bfloat16)

        blocks_in = current.reshape(ORDER // NB, NB, ORDER)
        lower_blocks = lower_panel.reshape(ORDER // NB, NB, NB)
        current = lax.map(update_rows, (blocks_in, lower_blocks)).reshape(ORDER, ORDER)
        current = current.at[:, first_row:after_row].set(jnp.where(below_mask, lower_panel, current[:, first_row:after_row]))
    return current.reshape(ROW_CYCLES, N_ROW * NB, COL_CYCLES, N_COL * NB)
```

```python
import functools

import jax
import jax.numpy as jnp
from jax import lax
from jax.experimental import pallas as pl
from jax.experimental.pallas import tpu as pltpu
from jax.sharding import PartitionSpec as P

NEWTON = 3
BF = jnp.bfloat16
F32 = jnp.float32
MESH = pl.DeviceIdType.MESH
VM = pltpu.VMEM


def dot(a, b):
    return jnp.dot(a, b, preferred_element_type=F32)


def dot_full(a, b):
    return jnp.dot(a, b, precision=lax.Precision.HIGHEST, preferred_element_type=F32)


def split3(x):
    hi = x.astype(BF)
    rest = x - hi.astype(F32)
    mid = rest.astype(BF)
    low = (rest - mid.astype(F32)).astype(BF)
    return hi, mid, low


def dot_bf_f32(a, parts):
    hi, mid, low = parts
    return dot(a, low) + dot(a, mid) + dot(a, hi)


def newton_inverse(diag):
    n = diag.shape[0]
    row = lax.broadcasted_iota(jnp.int32, (n, n), 0)
    col = lax.broadcasted_iota(jnp.int32, (n, n), 1)
    eye = jnp.where(row == col, 1.0, 0.0).astype(F32)
    approx = eye / 3.0
    for _ in range(NEWTON):
        product = dot_full(diag, approx)
        approx = dot_full(approx, 2.0 * eye - product)
    return approx


def interchange(pivots, nb):
    first, second = pivots[0], pivots[1]
    lane = jnp.arange(nb, dtype=jnp.int32)
    same = second[:, None] == first[None, :]
    source_two = jnp.where(
        jnp.any(same, axis=1), jnp.sum(jnp.where(same, lane[None, :], 0), axis=1), second
    )
    source = jnp.concatenate([first, source_two])
    back = (lane + nb)[:, None] == first[None, :]
    after = jnp.where(
        jnp.any(back, axis=1), jnp.sum(jnp.where(back, lane[None, :], 0), axis=1), lane + nb
    )
    after = jnp.concatenate([first, after])
    moved = (after - nb)[:, None] == lane[None, :]
    lifted = after[:, None] == second[None, :]
    target = jnp.where(
        jnp.any(moved, axis=1),
        jnp.sum(jnp.where(moved, second[None, :], 0), axis=1),
        jnp.where(
            jnp.any(lifted, axis=1),
            jnp.sum(jnp.where(lifted, lane[None, :] + nb, 0), axis=1),
            after,
        ),
    )
    return source, target


def pick_kernel(nr, where_ref, m_ref, first_ref, rest_ref, hot):
    c = pl.program_id(0)
    cycles, _, nb, _ = m_ref.shape
    rows = cycles * nb
    r = lax.axis_index("row")

    @pl.when(c == 0)
    def _():
        at = lax.broadcasted_iota(jnp.int32, (2 * nb, rows), 1)
        hot[...] = jnp.where(at == where_ref[...], 1.0, 0.0).astype(BF)

    block = m_ref[...].reshape(rows, nb)
    picked = dot(hot[...], block).astype(BF)
    top = block[:nb]
    zero = jnp.zeros_like(top)
    own = [jnp.where(r == s, top, zero) for s in range(2)]

    def put(ref):
        ref[0, : 2 * nb] = picked
        ref[0, 2 * nb : 3 * nb] = own[0]
        ref[0, 3 * nb :] = own[1]

    @pl.when(c == 0)
    def _():
        put(first_ref)

    @pl.when(c > 0)
    def _():
        put(rest_ref)


def pick(matrix, where, nr):
    ra, ca, nb, _ = matrix.shape
    return pl.pallas_call(
        functools.partial(pick_kernel, nr),
        grid=(ca,),
        in_specs=[
            pl.BlockSpec((2 * nb, 1), lambda c: (0, 0)),
            pl.BlockSpec((ra, 1, nb, nb), lambda c: (0, c, 0, 0)),
        ],
        out_specs=[
            pl.BlockSpec((1, 4 * nb, nb), lambda c: (0, 0, 0)),
            pl.BlockSpec((1, 4 * nb, nb), lambda c: (jnp.maximum(c - 1, 0), 0, 0)),
        ],
        out_shape=[
            jax.ShapeDtypeStruct((1, 4 * nb, nb), BF),
            jax.ShapeDtypeStruct((ca - 1, 4 * nb, nb), BF),
        ],
        scratch_shapes=[VM((2 * nb, ra * nb), BF)],
        name="pick_rows",
    )(where, matrix)


def limits(nz):
    far = nz // 2
    return {(0, 0): far, (0, 1): far - 1, (1, 0): far - 1, (1, 1): far}


class RingSum:
    @staticmethod
    def scratch(nc, nz, q, nb):
        far = nz // 2
        dma = pltpu.SemaphoreType.DMA
        return [
            VM((nz, 2, nc, q, nb), BF),
            VM((2, 2, far, nc, q, nb), BF),
            VM((2, 2, far, nc, q, nb), BF),
            dma((2, nz, 2)),
            dma((2, 2, 2, far)),
            dma((2, 2, 2, far)),
            dma((2, nz, 2)),
        ]

    def __init__(self, nz, c_ref, out_ref, scratch):
        self.nz, self.c, self.out = nz, c_ref, out_ref
        (self.pbuf, self.sbuf, self.rbuf, self.psem, self.rsem, self.gsem, self.qsem) = scratch
        r = lax.axis_index("row")
        self.z, self.k = r // 2, r % 2
        self.partner = self.z * 2 + (1 - self.k)
        self.next = [
            ((self.z + nz - 1) % nz) * 2 + self.k,
            ((self.z + 1) % nz) * 2 + self.k,
        ]

    def peers(self):
        return [{"row": self.partner}, {"row": self.next[0]}, {"row": self.next[1]}]

    def at(self, offset):
        return (self.z + offset) % self.nz

    def copy(self, src, dst, send, recv, target):
        return pltpu.make_async_remote_copy(
            src_ref=src, dst_ref=dst, send_sem=send, recv_sem=recv,
            device_id={"row": target}, device_id_type=MESH,
        )

    def pair(self, slot, sub):
        t = self.at(slot)
        return self.copy(
            self.c.at[:, 1 - self.k, t, sub], self.pbuf.at[slot, sub],
            self.psem.at[0, slot, sub], self.psem.at[1, slot, sub], self.partner,
        )

    def reduce(self, way, sub, d):
        i = d - 1
        return self.copy(
            self.sbuf.at[way, sub, i], self.rbuf.at[way, sub, i],
            self.rsem.at[0, way, sub, i], self.rsem.at[1, way, sub, i], self.next[way],
        )

    def slot(self, way, d):
        return d % self.nz if way == 0 else (self.nz - d) % self.nz

    def spread(self, way, sub, d):
        t = self.at(self.slot(way, d - 1))
        i = d - 1
        piece = self.out.at[:, self.k, t, sub]
        return self.copy(
            piece, piece, self.gsem.at[0, way, sub, i], self.gsem.at[1, way, sub, i], self.next[way]
        )

    def arrived(self, way, sub, d):
        t = self.at(self.slot(way, d))
        i = d - 1
        piece = self.out.at[:, self.k, t, sub]
        self.copy(
            piece, piece, self.gsem.at[0, way, sub, i], self.gsem.at[1, way, sub, i], self.next[way]
        ).wait_recv()

    def share(self, slot, sub, core):
        piece = self.out.at[:, core, self.at(slot), sub]
        return self.copy(
            piece, piece, self.qsem.at[0, slot, sub], self.qsem.at[1, slot, sub], self.partner
        )

    def steps(self):
        nz, far, limit = self.nz, self.nz // 2, limits(self.nz)
        order = []
        for d in range(far, 0, -1):
            for slot in (self.slot(1, d), self.slot(0, d)):
                if slot not in order:
                    order.append(slot)
        order.append(0)
        for slot in order:
            for sub in range(2):
                self.pair(slot, sub).start()
        yield
        for d in range(far, 0, -1):
            for way, sub in limit:
                if d > limit[way, sub]:
                    continue
                slot = self.slot(1 - way, d)
                if not (d == far or (way == 1 and d == far)):
                    pass
                self.pair_once(slot, sub)
                value = self.c[:, self.k, self.at(slot), sub] + self.pbuf[slot, sub]
                if d < limit[way, sub]:
                    self.reduce(way, sub, d + 1).wait_recv()
                    value = value + self.rbuf[way, sub, d]
                self.sbuf[way, sub, d - 1] = value
                self.reduce(way, sub, d).start()
            yield
        for sub in range(2):
            self.pair_once(0, sub)
            value = self.c[:, self.k, self.z, sub] + self.pbuf[0, sub]
            for way in range(2):
                if limit[way, sub] >= 1:
                    self.reduce(way, sub, 1).wait_recv()
                    value = value + self.rbuf[way, sub, 0]
            self.out[:, self.k, self.z, sub] = value
            for way in range(2):
                if limit[way, sub] >= 1:
                    self.spread(way, sub, 1).start()
            self.share(0, sub, self.k).start()
        yield
        for d in range(1, far + 1):
            for way, sub in limit:
                if d > limit[way, sub]:
                    continue
                self.arrived(way, sub, d)
                if d < limit[way, sub]:
                    self.spread(way, sub, d + 1).start()
                self.share(self.slot(way, d), sub, self.k).start()
            yield
        for slot in range(nz):
            for sub in range(2):
                self.share(slot, sub, 1 - self.k).wait_recv()
        for slot in range(nz):
            for sub in range(2):
                self.pair(slot, sub).wait_send()
                self.share(slot, sub, self.k).wait_send()
        for (way, sub), top in limit.items():
            for d in range(1, top + 1):
                self.reduce(way, sub, d).wait_send()
                self.spread(way, sub, d).wait_send()

    seen = None

    def pair_once(self, slot, sub):
        if self.seen is None:
            self.seen = set()
        if (slot, sub) not in self.seen:
            self.seen.add((slot, sub))
            self.pair(slot, sub).wait_recv()


class PanelRelay:
    @staticmethod
    def scratch(parts):
        dma = pltpu.SemaphoreType.DMA
        return [dma((3, 2, 2, parts)), dma((2,))]

    def __init__(self, nx, ny, parts, src_ref, out_ref, scratch):
        self.nx, self.ny, self.parts = nx, ny, parts
        self.src, self.out = src_ref, out_ref
        self.sem, self.own_sem = scratch
        c = lax.axis_index("col")
        self.c, self.x, self.y = c, c // ny, c % ny
        self.height = src_ref.shape[0] // (2 * parts)

    def neighbours(self, way):
        nx, ny, x, y = self.nx, self.ny, self.x, self.y
        if way:
            return (x + 1) % nx * ny + y, x * ny + (y + 1) % ny
        return (x + nx - 1) % nx * ny + y, x * ny + (y + ny - 1) % ny

    def peers(self):
        return [{"col": n} for way in range(2) for n in self.neighbours(way)]

    def place(self, root, way):
        x0, y0 = root // self.ny, root % self.ny
        if way:
            return (self.x + self.nx - x0) % self.nx, (self.y + self.ny - y0) % self.ny
        return (x0 + self.nx - self.x) % self.nx, (y0 + self.ny - self.y) % self.ny

    def copy(self, root, way, part, axis):
        start = (way * self.parts + part) * self.height
        piece = self.out.at[root, pl.ds(start, self.height)]
        return pltpu.make_async_remote_copy(
            src_ref=piece, dst_ref=piece,
            send_sem=self.sem.at[axis, root, way, part],
            recv_sem=self.sem.at[2, root, way, part],
            device_id={"col": self.neighbours(way)[axis]}, device_id_type=MESH,
        )

    def sends(self, root, way, part, act):
        h, v = self.place(root, way)

        @pl.when(jnp.logical_and(v == 0, h < self.nx - 1))
        def _():
            act(self.copy(root, way, part, 0))

        @pl.when(v < self.ny - 1)
        def _():
            act(self.copy(root, way, part, 1))

    def steps(self):
        for root in range(2):
            @pl.when(self.c == root)
            def _():
                own = pltpu.make_async_copy(self.src, self.out.at[root], self.own_sem.at[root])
                own.start()
                own.wait()
        yield
        for part in range(self.parts):
            for root in range(2):
                for way in range(2):
                    @pl.when(self.c != root)
                    def _():
                        self.copy(root, way, part, 0).wait_recv()

                    self.sends(root, way, part, lambda copy: copy.start())
            yield
        for part in range(self.parts):
            for root in range(2):
                for way in range(2):
                    self.sends(root, way, part, lambda copy: copy.wait_send())


def greet(peers):
    barrier = pltpu.get_barrier_semaphore()
    for peer in peers:
        pl.semaphore_signal(barrier, inc=1, device_id=peer, device_id_type=MESH)
    pl.semaphore_wait(barrier, len(peers))


def run_all(plans):
    plans = list(plans)
    while plans:
        plans = [plan for plan in plans if next(plan, plan) is not plan]


def ring_kernel(nz, c_ref, out_ref, *scratch):
    ring = RingSum(nz, c_ref, out_ref, scratch)
    greet(ring.peers())
    run_all([ring.steps()])


def params(ident):
    return pltpu.CompilerParams(
        collective_id=ident, has_side_effects=True, vmem_limit_bytes=48 << 20
    )


def ring_sum(parts, nz, ident):
    nc, rows, nb = parts.shape
    q = rows // (4 * nz)
    shape = (nc, 2, nz, 2, q, nb)
    out = pl.pallas_call(
        functools.partial(ring_kernel, nz),
        out_shape=jax.ShapeDtypeStruct(shape, BF),
        in_specs=[pl.BlockSpec(memory_space=VM)],
        out_specs=pl.BlockSpec(memory_space=VM),
        scratch_shapes=RingSum.scratch(nc, nz, q, nb),
        compiler_params=params(ident),
        name="ring_sum",
    )(parts.reshape(shape))
    return out.reshape(nc, rows, nb)


def both_kernel(nz, nx, ny, parts, c_ref, src_ref, out_ref, panel_ref, *scratch):
    ring = RingSum(nz, c_ref, out_ref, scratch[:7])
    relay = PanelRelay(nx, ny, parts, src_ref, panel_ref, scratch[7:])
    greet(ring.peers() + relay.peers())
    run_all([relay.steps(), ring.steps()])


def ring_and_relay(rest, src, nz, nx, ny, parts, ident):
    nc, rows, nb = rest.shape
    q = rows // (4 * nz)
    shape = (nc, 2, nz, 2, q, nb)
    out, panel = pl.pallas_call(
        functools.partial(both_kernel, nz, nx, ny, parts),
        out_shape=[
            jax.ShapeDtypeStruct(shape, BF),
            jax.ShapeDtypeStruct((2,) + src.shape, BF),
        ],
        in_specs=[pl.BlockSpec(memory_space=VM)] * 2,
        out_specs=[pl.BlockSpec(memory_space=VM)] * 2,
        scratch_shapes=RingSum.scratch(nc, nz, q, nb) + PanelRelay.scratch(parts),
        compiler_params=params(ident),
        name="ring_and_relay",
    )(rest.reshape(shape), src)
    return out.reshape(nc, rows, nb), panel


def hot_rows(at_ref, a, nb):
    row = lax.broadcasted_iota(jnp.int32, (nb, 2 * nb), 0) + a * nb
    hot = jnp.where(row == at_ref[...], 1.0, 0.0)
    return hot.astype(BF), jnp.sum(hot, axis=1, keepdims=True) > 0.0


def panel_kernel(at_ref, m_ref, rows_ref, out_ref):
    cycles, _, nb, _ = m_ref.shape
    r = lax.axis_index("row")
    old = rows_ref[0, 2 * nb :]
    for a in range(cycles):
        hot, hit = hot_rows(at_ref, a, nb)
        value = jnp.where(hit, dot(hot, old).astype(BF), m_ref[a, 0])
        if a == 0:
            value = jnp.where(r == 0, rows_ref[0, :nb], value)
            value = jnp.where(r == 1, rows_ref[0, nb : 2 * nb], value)
        out_ref[a * nb : (a + 1) * nb] = value
    out_ref[cycles * nb :] = rows_ref[0, : 2 * nb]


def panel_rows(matrix, at, rows):
    ra, ca, nb, _ = matrix.shape
    return pl.pallas_call(
        panel_kernel,
        grid=(1,),
        in_specs=[
            pl.BlockSpec((1, 2 * nb), lambda i: (0, 0)),
            pl.BlockSpec((ra, 1, nb, nb), lambda i: (0, 0, 0, 0)),
            pl.BlockSpec((1, 4 * nb, nb), lambda i: (0, 0, 0)),
        ],
        out_specs=pl.BlockSpec(((ra + 2) * nb, nb), lambda i: (0, 0)),
        out_shape=jax.ShapeDtypeStruct(((ra + 2) * nb, nb), BF),
        name="panel_rows",
    )(at, matrix, rows)


def update_kernel(
    nr, at_ref, m_ref, first_ref, rest_ref, panel_ref, top_ref, out_ref, upper, inv, corner
):
    a = pl.program_id(0)
    _, nc, nb, _ = m_ref.shape
    r = lax.axis_index("row")
    col = lax.axis_index("col")

    def rows_of(c):
        return first_ref.at[0] if c == 0 else rest_ref.at[c - 1]

    @pl.when(a == 0)
    def _():
        inverse = split3(newton_inverse(top_ref[0, :nb].astype(F32)))
        for i in range(3):
            inv[0, i] = inverse[i]
        lower = dot_bf_f32(top_ref[0, nb:], inverse).astype(BF)
        corner[...] = top_ref[1, :nb]
        diag = (top_ref[1, nb:].astype(F32) - dot(lower, top_ref[1, :nb])).astype(BF)
        inverse = split3(newton_inverse(diag.astype(F32)))
        for i in range(3):
            inv[1, i] = inverse[i]
        for c in range(nc):
            one = rows_of(c)[:nb]
            if c == 0:
                one = jnp.where(col == 0, jnp.zeros_like(one), one)
            two = (rows_of(c)[nb : 2 * nb].astype(F32) - dot(lower, one)).astype(BF)
            if c == 0:
                two = jnp.where(col <= 1, jnp.zeros_like(two), two)
            upper[0, c] = one
            upper[1, c] = two

    zero = jnp.zeros((nb, nb), BF)
    block = a * nr + r
    lower0 = dot_bf_f32(panel_ref[0], [inv[0, i] for i in range(3)]).astype(BF)
    lower0 = jnp.where(block >= 1, lower0, zero)
    second = (panel_ref[1].astype(F32) - dot(lower0, corner[...])).astype(BF)
    lower1 = dot_bf_f32(second, [inv[1, i] for i in range(3)]).astype(BF)
    lower1 = jnp.where(block >= 2, lower1, zero)
    hot, hit = hot_rows(at_ref, a, nb)
    for c in range(nc):
        value = jnp.where(hit, dot(hot, rows_of(c)[2 * nb :]).astype(BF), m_ref[0, c])
        value = jnp.where(block == 0, rows_of(c)[:nb], value)
        value = jnp.where(block == 1, rows_of(c)[nb : 2 * nb], value)
        value = (value.astype(F32) - dot(lower0, upper[0, c])).astype(BF)
        value = (value.astype(F32) - dot(lower1, upper[1, c])).astype(BF)
        if c == 0:
            value = jnp.where(jnp.logical_and(col == 0, block >= 1), lower0, value)
            value = jnp.where(jnp.logical_and(col == 1, block >= 2), lower1, value)
        out_ref[0, c] = value


def update(matrix, at, first, rest, panel, nr):
    ra, ca, nb, _ = matrix.shape
    return pl.pallas_call(
        functools.partial(update_kernel, nr),
        grid=(ra,),
        in_specs=[
            pl.BlockSpec((1, 2 * nb), lambda a: (0, 0)),
            pl.BlockSpec((1, ca, nb, nb), lambda a: (a, 0, 0, 0)),
            pl.BlockSpec(first.shape, lambda a: (0, 0, 0)),
            pl.BlockSpec(rest.shape, lambda a: (0, 0, 0)),
            pl.BlockSpec((2, nb, nb), lambda a: (0, a, 0)),
            pl.BlockSpec((2, 2 * nb, nb), lambda a: (0, 0, 0)),
        ],
        out_specs=pl.BlockSpec((1, ca, nb, nb), lambda a: (a, 0, 0, 0)),
        out_shape=jax.ShapeDtypeStruct(matrix.shape, BF),
        scratch_shapes=[
            VM((2, ca, nb, nb), BF),
            VM((2, 3, nb, nb), BF),
            VM((nb, nb), BF),
        ],
        compiler_params=pltpu.CompilerParams(vmem_limit_bytes=48 << 20),
        name="update",
    )(at, matrix, first, rest, panel, panel[:, ra * nb :])


def body(nr, nx, ny, parts, matrix, pivots):
    r = lax.axis_index("row")
    matrix = matrix.transpose(0, 2, 1, 3)
    nb = matrix.shape[2]
    source, target = interchange(pivots, nb)

    def local(rows, valid):
        index = rows // (nb * nr) * nb + rows % nb
        return jnp.where(jnp.logical_and(valid, rows // nb % nr == r), index, -1)

    where = local(source, True)[:, None]
    at = local(target, target >= 2 * nb)[None, :]
    first, rest = pick(matrix, where, nr)
    first = ring_sum(first, nr // 2, 1)
    src = panel_rows(matrix, at, first)
    rest, panel = ring_and_relay(rest, src, nr // 2, nx, ny, parts, 2)
    out = update(matrix, at, first, rest, panel, nr)
    return out.transpose(0, 2, 1, 3)


def solution(mesh):
    nr, ncol = mesh.shape["row"], mesh.shape["col"]
    ny = int(ncol**0.5)
    return jax.shard_map(
        functools.partial(body, nr, ncol // ny, ny, 8),
        mesh=mesh,
        in_specs=(P(None, "row", None, "col"), P()),
        out_specs=P(None, "row", None, "col"),
        check_vma=False,
    )
```

```python
import functools

import jax
import jax.numpy as jnp
from jax import lax
from jax.experimental import pallas as pl
from jax.experimental.pallas import tpu as pltpu
from jax.sharding import PartitionSpec as P

NEWTON = 3
BF = jnp.bfloat16
F32 = jnp.float32
MESH = pl.DeviceIdType.MESH
VM = pltpu.VMEM


def dot(a, b):
    return jnp.dot(a, b, preferred_element_type=F32)


def dot_full(a, b):
    return jnp.dot(a, b, precision=lax.Precision.HIGHEST, preferred_element_type=F32)


def split3(x):
    hi = x.astype(BF)
    rest = x - hi.astype(F32)
    mid = rest.astype(BF)
    low = (rest - mid.astype(F32)).astype(BF)
    return hi, mid, low


def dot_bf_f32(a, parts):
    hi, mid, low = parts
    return dot(a, low) + dot(a, mid) + dot(a, hi)


def newton_inverse(diag):
    n = diag.shape[0]
    row = lax.broadcasted_iota(jnp.int32, (n, n), 0)
    col = lax.broadcasted_iota(jnp.int32, (n, n), 1)
    eye = jnp.where(row == col, 1.0, 0.0).astype(F32)
    approx = eye / 3.0
    for _ in range(NEWTON):
        product = dot_full(diag, approx)
        approx = dot_full(approx, 2.0 * eye - product)
    return approx


def interchange(pivots, nb):
    first, second = pivots[0], pivots[1]
    lane = jnp.arange(nb, dtype=jnp.int32)
    same = second[:, None] == first[None, :]
    source_two = jnp.where(
        jnp.any(same, axis=1), jnp.sum(jnp.where(same, lane[None, :], 0), axis=1), second
    )
    source = jnp.concatenate([first, source_two])
    back = (lane + nb)[:, None] == first[None, :]
    after = jnp.where(
        jnp.any(back, axis=1), jnp.sum(jnp.where(back, lane[None, :], 0), axis=1), lane + nb
    )
    after = jnp.concatenate([first, after])
    moved = (after - nb)[:, None] == lane[None, :]
    lifted = after[:, None] == second[None, :]
    target = jnp.where(
        jnp.any(moved, axis=1),
        jnp.sum(jnp.where(moved, second[None, :], 0), axis=1),
        jnp.where(
            jnp.any(lifted, axis=1),
            jnp.sum(jnp.where(lifted, lane[None, :] + nb, 0), axis=1),
            after,
        ),
    )
    return source, target


def pick_kernel(where_ref, m_ref, first_ref, rest_ref, src_ref, hot):
    c = pl.program_id(0)
    cycles, _, nb, _ = m_ref.shape
    rows = cycles * nb
    r = lax.axis_index("row")

    @pl.when(c == 0)
    def _():
        at = lax.broadcasted_iota(jnp.int32, (2 * nb, rows), 1)
        hot[...] = jnp.where(at == where_ref[...], 1.0, 0.0).astype(BF)

    block = m_ref[...].reshape(rows, nb)
    picked = dot(hot[...], block).astype(BF)
    top = block[:nb]
    zero = jnp.zeros_like(top)
    own = [jnp.where(r == s, top, zero) for s in range(2)]

    def put(ref):
        ref[0, : 2 * nb] = picked
        ref[0, 2 * nb : 3 * nb] = own[0]
        ref[0, 3 * nb :] = own[1]

    @pl.when(c == 0)
    def _():
        put(first_ref)
        src_ref[0] = block[:, : nb // 2]
        src_ref[1] = block[:, nb // 2 :]

    @pl.when(c > 0)
    def _():
        put(rest_ref)


def pick(matrix, where):
    ra, ca, nb, _ = matrix.shape
    return pl.pallas_call(
        pick_kernel,
        grid=(ca,),
        in_specs=[
            pl.BlockSpec((2 * nb, 1), lambda c: (0, 0)),
            pl.BlockSpec((ra, 1, nb, nb), lambda c: (0, c, 0, 0)),
        ],
        out_specs=[
            pl.BlockSpec((1, 4 * nb, nb), lambda c: (0, 0, 0)),
            pl.BlockSpec((1, 4 * nb, nb), lambda c: (jnp.maximum(c - 1, 0), 0, 0)),
            pl.BlockSpec((2, ra * nb, nb // 2), lambda c: (0, 0, 0)),
        ],
        out_shape=[
            jax.ShapeDtypeStruct((1, 4 * nb, nb), BF),
            jax.ShapeDtypeStruct((ca - 1, 4 * nb, nb), BF),
            jax.ShapeDtypeStruct((2, ra * nb, nb // 2), BF),
        ],
        scratch_shapes=[VM((2 * nb, ra * nb), BF)],
        name="pick_rows",
    )(where, matrix)


def limits(nz):
    far = nz // 2
    return {(0, 0): far, (0, 1): far - 1, (1, 0): far - 1, (1, 1): far}


class RingSum:
    @staticmethod
    def scratch(nc, nz, q, nb):
        far = nz // 2
        dma = pltpu.SemaphoreType.DMA
        return [
            VM((nz, 2, nc, q, nb), BF),
            VM((2, 2, far, nc, q, nb), BF),
            VM((2, 2, far, nc, q, nb), BF),
            dma((2, nz, 2)),
            dma((2, 2, 2, far)),
            dma((2, 2, 2, far)),
            dma((2, nz, 2)),
        ]

    def __init__(self, nz, c_ref, out_ref, scratch):
        self.nz, self.c, self.out = nz, c_ref, out_ref
        (self.pbuf, self.sbuf, self.rbuf, self.psem, self.rsem, self.gsem, self.qsem) = scratch
        r = lax.axis_index("row")
        self.z, self.k = r // 2, r % 2
        self.partner = self.z * 2 + (1 - self.k)
        self.next = [
            ((self.z + nz - 1) % nz) * 2 + self.k,
            ((self.z + 1) % nz) * 2 + self.k,
        ]

    def peers(self):
        return [{"row": self.partner}, {"row": self.next[0]}, {"row": self.next[1]}]

    def at(self, offset):
        return (self.z + offset) % self.nz

    def copy(self, src, dst, send, recv, target):
        return pltpu.make_async_remote_copy(
            src_ref=src, dst_ref=dst, send_sem=send, recv_sem=recv,
            device_id={"row": target}, device_id_type=MESH,
        )

    def pair(self, slot, sub):
        t = self.at(slot)
        return self.copy(
            self.c.at[:, 1 - self.k, t, sub], self.pbuf.at[slot, sub],
            self.psem.at[0, slot, sub], self.psem.at[1, slot, sub], self.partner,
        )

    def reduce(self, way, sub, d):
        i = d - 1
        return self.copy(
            self.sbuf.at[way, sub, i], self.rbuf.at[way, sub, i],
            self.rsem.at[0, way, sub, i], self.rsem.at[1, way, sub, i], self.next[way],
        )

    def slot(self, way, d):
        return d % self.nz if way == 0 else (self.nz - d) % self.nz

    def spread(self, way, sub, d):
        t = self.at(self.slot(way, d - 1))
        i = d - 1
        piece = self.out.at[:, self.k, t, sub]
        return self.copy(
            piece, piece, self.gsem.at[0, way, sub, i], self.gsem.at[1, way, sub, i], self.next[way]
        )

    def arrived(self, way, sub, d):
        t = self.at(self.slot(way, d))
        i = d - 1
        piece = self.out.at[:, self.k, t, sub]
        self.copy(
            piece, piece, self.gsem.at[0, way, sub, i], self.gsem.at[1, way, sub, i], self.next[way]
        ).wait_recv()

    def share(self, slot, sub, core):
        piece = self.out.at[:, core, self.at(slot), sub]
        return self.copy(
            piece, piece, self.qsem.at[0, slot, sub], self.qsem.at[1, slot, sub], self.partner
        )

    def steps(self):
        nz, far, limit = self.nz, self.nz // 2, limits(self.nz)
        order = []
        for d in range(far, 0, -1):
            for slot in (self.slot(1, d), self.slot(0, d)):
                if slot not in order:
                    order.append(slot)
        order.append(0)
        for slot in order:
            for sub in range(2):
                self.pair(slot, sub).start()
        yield
        for d in range(far, 0, -1):
            for way, sub in limit:
                if d > limit[way, sub]:
                    continue
                slot = self.slot(1 - way, d)
                self.pair_once(slot, sub)
                value = self.c[:, self.k, self.at(slot), sub] + self.pbuf[slot, sub]
                if d < limit[way, sub]:
                    self.reduce(way, sub, d + 1).wait_recv()
                    value = value + self.rbuf[way, sub, d]
                self.sbuf[way, sub, d - 1] = value
                self.reduce(way, sub, d).start()
            yield
        for sub in range(2):
            self.pair_once(0, sub)
            value = self.c[:, self.k, self.z, sub] + self.pbuf[0, sub]
            for way in range(2):
                if limit[way, sub] >= 1:
                    self.reduce(way, sub, 1).wait_recv()
                    value = value + self.rbuf[way, sub, 0]
            self.out[:, self.k, self.z, sub] = value
            for way in range(2):
                if limit[way, sub] >= 1:
                    self.spread(way, sub, 1).start()
            self.share(0, sub, self.k).start()
        yield
        for d in range(1, far + 1):
            for way, sub in limit:
                if d > limit[way, sub]:
                    continue
                self.arrived(way, sub, d)
                if d < limit[way, sub]:
                    self.spread(way, sub, d + 1).start()
                self.share(self.slot(way, d), sub, self.k).start()
            yield
        for slot in range(nz):
            for sub in range(2):
                self.share(slot, sub, 1 - self.k).wait_recv()
        for slot in range(nz):
            for sub in range(2):
                self.pair(slot, sub).wait_send()
                self.share(slot, sub, self.k).wait_send()
        for (way, sub), top in limit.items():
            for d in range(1, top + 1):
                self.reduce(way, sub, d).wait_send()
                self.spread(way, sub, d).wait_send()

    seen = None

    def pair_once(self, slot, sub):
        if self.seen is None:
            self.seen = set()
        if (slot, sub) not in self.seen:
            self.seen.add((slot, sub))
            self.pair(slot, sub).wait_recv()


class PlaneCast:
    @staticmethod
    def scratch(nx, ny):
        dma = pltpu.SemaphoreType.DMA
        far = max(nx, ny) // 2
        return [dma((nx * ny,)), dma((2,)), dma((2, 2, 2, 2, far)), dma((2,))]

    def __init__(self, nx, ny, src_ref, out_ref, scratch):
        self.n, self.src, self.out = (nx, ny), src_ref, out_ref
        self.far_sem, self.near_sem, self.ring_sem, self.share_sem = scratch
        self.c = lax.axis_index("col")
        self.pos = self.c // ny, self.c % ny

    def step(self, axis, way):
        x, y = self.pos
        nx, ny = self.n
        if axis == 0:
            return (x + (1 if way else nx - 1)) % nx * ny + y
        return x * ny + (y + (1 if way else ny - 1)) % ny

    def peers(self):
        nx, ny = self.n
        found = [{"col": self.step(axis, way)} for axis in range(2) for way in range(2)]
        return found

    def copy(self, src, dst, send, recv, target):
        return pltpu.make_async_remote_copy(
            src_ref=src, dst_ref=dst, send_sem=send, recv_sem=recv,
            device_id={"col": target}, device_id_type=MESH,
        )

    def far(self, i):
        nx, ny = self.n
        t = (self.c + i) % (nx * ny)
        return self.copy(
            self.src.at[:, t // ny, t % ny], self.out.at[self.c, :, t // ny, t % ny],
            self.far_sem.at[i], self.near_sem.at[self.c], t,
        )

    def keep(self):
        x, y = self.pos
        self.out[self.c, :, x, y] = self.src[:, x, y]

    def near(self, root):
        piece = self.out.at[root, :, self.pos[0], self.pos[1]]
        return self.copy(piece, piece, self.far_sem.at[0], self.near_sem.at[root], root)

    def piece(self, half, phase, q, roots):
        axis = half if phase == 0 else 1 - half
        if phase == 1:
            if axis == 0:
                return self.out.at[roots, half, q]
            return self.out.at[roots, half, :, q]
        if axis == 0:
            return self.out.at[roots, half, q, self.pos[1]]
        return self.out.at[roots, half, self.pos[0], q]

    def ring(self, half, phase, way, d, origin):
        axis = half if phase == 0 else 1 - half
        n = self.n[axis]
        roots = slice(None) if d < n // 2 else way
        q = (self.pos[axis] + (origin if way == 0 else n - origin)) % n
        piece = self.piece(half, phase, q, roots)
        sem = self.ring_sem
        return self.copy(
            piece, piece, sem.at[0, half, phase, way, d - 1], sem.at[1, half, phase, way, d - 1],
            self.step(axis, way),
        )

    def kinds(self, phase):
        for half in range(2):
            for way in range(2):
                yield half, way, self.n[half if phase == 0 else 1 - half] // 2

    def steps(self):
        total = self.n[0] * self.n[1]

        @pl.when(self.c < 2)
        def _():
            for i in range(total - 1, 0, -1):
                self.far(i).start()

        yield
        for root in range(2):
            @pl.when(self.c != root)
            def _():
                self.near(root).wait_recv()

        for phase in range(2):
            top = 0
            for half, way, far in self.kinds(phase):
                self.ring(half, phase, way, 1, 0).start()
                top = max(top, far)
            for d in range(1, top + 1):
                yield
                for half, way, far in self.kinds(phase):
                    if d <= far:
                        self.ring(half, phase, way, d, d).wait_recv()
                    if d < far:
                        if d + 1 < far:
                            self.ring(half, phase, way, d + 1, d).start()
                        else:
                            self.ring(half, phase, way, d + 1, d).start()
        yield

        @pl.when(self.c < 2)
        def _():
            for i in range(total - 1, 0, -1):
                self.far(i).wait_send()

        for phase in range(2):
            for half, way, far in self.kinds(phase):
                for d in range(1, far + 1):
                    self.ring(half, phase, way, d, d - 1).wait_send()


def greet(peers):
    barrier = pltpu.get_barrier_semaphore()
    for peer in peers:
        pl.semaphore_signal(barrier, inc=1, device_id=peer, device_id_type=MESH)
    pl.semaphore_wait(barrier, len(peers))


def params(ident):
    return pltpu.CompilerParams(
        collective_id=ident, has_side_effects=True, vmem_limit_bytes=48 << 20
    )


def exchange_kernel(
    nz, nx, ny, first_ref, rest_ref, src_ref, first_out, rest_out, panel_out, top_out, *scratch
):
    half = rest_ref.shape[0] // 2
    slow = rest_ref.shape[0] - half
    rings = [
        RingSum(nz, first_ref, first_out, scratch[:7]),
        RingSum(nz, rest_ref.at[:slow], rest_out.at[:slow], scratch[7:14]),
    ]
    rest = scratch[14:]
    if half:
        rings.append(RingSum(nz, rest_ref.at[slow:], rest_out.at[slow:], scratch[14:21]))
        rest = scratch[21:]
    core = rings[0].k
    panel = PlaneCast(nx, ny, src_ref, panel_out, rest[:4])
    stage = rest[8]
    top = PlaneCast(nx, ny, stage, top_out.at[core], rest[4:8])
    col = panel.c
    total = nx * ny
    lanes = src_ref.shape[-1]

    @pl.when(col < 2)
    def _():
        panel.keep()

    corners = [{"col": (col + i) % total} for i in range(1, total)]
    greet(rings[0].peers() + corners)

    def top_steps():
        @pl.when(col < 2)
        def _():
            for sub in range(2):
                part = first_out[0, core, :, :, :, sub * lanes : (sub + 1) * lanes]
                stage[sub] = part.reshape(stage.shape[1:])
            top.keep()

        yield from top.steps()
        mine, other = top_out.at[core], top_out.at[1 - core]

        def share(ref):
            return rings[0].copy(
                ref, ref, top.share_sem.at[0], top.share_sem.at[1], rings[0].partner
            )

        share(mine).start()
        share(other).wait_recv()
        share(mine).wait_send()

    plans = {"X": panel.steps(), "T": top_steps()}
    for name, ring in zip("FAB", rings):
        plans[name] = ring.steps()
    for name in ORDER:
        if name in plans:
            next(plans[name], None)
    for name in "FTXAB":
        if name in plans:
            for _ in plans[name]:
                pass


ORDER = "XFABFFABFFXABFFXABFFXABFFXTABTXABTXABTABTAB"


def exchange(first, rest, src, nz, nx, ny, ident):
    nc, rows, nb = rest.shape
    q = rows // (4 * nz)
    half = nc // 2
    total = nx * ny

    def grid(n):
        return (n, 2, nz, 2, q, nb)

    wide = src.shape[1]
    plane = (2, nx, ny, wide // total, nb // 2)
    corner = (2, 2, 2, nx, ny, 2 * nb // total, nb // 2)
    scratch = RingSum.scratch(1, nz, q, nb) + RingSum.scratch(nc - half, nz, q, nb)
    if half:
        scratch += RingSum.scratch(half, nz, q, nb)
    scratch += PlaneCast.scratch(nx, ny) + PlaneCast.scratch(nx, ny)
    scratch.append(VM(corner[2:], BF))
    first, rest, panel, top = pl.pallas_call(
        functools.partial(exchange_kernel, nz, nx, ny),
        out_shape=[
            jax.ShapeDtypeStruct(grid(1), BF),
            jax.ShapeDtypeStruct(grid(nc), BF),
            jax.ShapeDtypeStruct((2,) + plane, BF),
            jax.ShapeDtypeStruct(corner, BF),
        ],
        in_specs=[pl.BlockSpec(memory_space=VM)] * 3,
        out_specs=[pl.BlockSpec(memory_space=VM)] * 4,
        scratch_shapes=scratch,
        compiler_params=params(ident),
        name="exchange",
    )(first.reshape(grid(1)), rest.reshape(grid(nc)), src.reshape(plane))
    return (
        first.reshape(1, rows, nb),
        rest.reshape(nc, rows, nb),
        panel.reshape(2, 2, wide, nb // 2),
        top.reshape(2, 2, 2, 2 * nb, nb // 2),
    )


def hot_rows(at_ref, a, nb):
    row = lax.broadcasted_iota(jnp.int32, (nb, 2 * nb), 0) + a * nb
    hot = jnp.where(row == at_ref[...], 1.0, 0.0)
    return hot.astype(BF), jnp.sum(hot, axis=1, keepdims=True) > 0.0


def update_kernel(
    nr, at_ref, m_ref, first_ref, rest_ref, panel_ref, top_ref, out_ref, upper, inv, heads
):
    a = pl.program_id(0)
    _, nc, nb, _ = m_ref.shape
    r = lax.axis_index("row")
    col = lax.axis_index("col")

    def rows_of(c):
        return first_ref.at[0] if c == 0 else rest_ref.at[c - 1]

    def whole(ref, *at):
        return jnp.concatenate([ref[at + (0,)], ref[at + (1,)]], axis=-1)

    @pl.when(a == 0)
    def _():
        for i in range(2):
            for root in range(2):
                heads[i, root] = whole(top_ref, i, root)
        inverse = split3(newton_inverse(heads[0, 0, :nb].astype(F32)))
        for i in range(3):
            inv[0, i] = inverse[i]
        lower = dot_bf_f32(heads[0, 0, nb:], inverse).astype(BF)
        diag = (heads[0, 1, nb:].astype(F32) - dot(lower, heads[0, 1, :nb])).astype(BF)
        inverse = split3(newton_inverse(diag.astype(F32)))
        for i in range(3):
            inv[1, i] = inverse[i]
        for c in range(nc):
            one = rows_of(c)[:nb]
            if c == 0:
                one = jnp.where(col == 0, jnp.zeros_like(one), one)
            two = (rows_of(c)[nb : 2 * nb].astype(F32) - dot(lower, one)).astype(BF)
            if c == 0:
                two = jnp.where(col <= 1, jnp.zeros_like(two), two)
            upper[0, c] = one
            upper[1, c] = two

    zero = jnp.zeros((nb, nb), BF)
    block = a * nr + r
    hot, hit = hot_rows(at_ref, a, nb)

    def swapped(old, top, mine):
        value = jnp.where(hit, dot(hot, old).astype(BF), mine)
        value = jnp.where(block == 0, top[:nb], value)
        return jnp.where(block == 1, top[nb:], value)

    panels = [swapped(heads[1, p], heads[0, p], whole(panel_ref, p)) for p in range(2)]
    lower0 = dot_bf_f32(panels[0], [inv[0, i] for i in range(3)]).astype(BF)
    lower0 = jnp.where(block >= 1, lower0, zero)
    second = (panels[1].astype(F32) - dot(lower0, heads[0, 1, :nb])).astype(BF)
    lower1 = dot_bf_f32(second, [inv[1, i] for i in range(3)]).astype(BF)
    lower1 = jnp.where(block >= 2, lower1, zero)
    for c in range(nc):
        value = swapped(rows_of(c)[2 * nb :], rows_of(c)[: 2 * nb], m_ref[0, c])
        value = (value.astype(F32) - dot(lower0, upper[0, c])).astype(BF)
        value = (value.astype(F32) - dot(lower1, upper[1, c])).astype(BF)
        if c == 0:
            value = jnp.where(jnp.logical_and(col == 0, block >= 1), lower0, value)
            value = jnp.where(jnp.logical_and(col == 1, block >= 2), lower1, value)
        out_ref[0, c] = value


def update(matrix, at, first, rest, panel, top, nr):
    ra, ca, nb, _ = matrix.shape
    return pl.pallas_call(
        functools.partial(update_kernel, nr),
        grid=(ra,),
        in_specs=[
            pl.BlockSpec((1, 2 * nb), lambda a: (0, 0)),
            pl.BlockSpec((1, ca, nb, nb), lambda a: (a, 0, 0, 0)),
            pl.BlockSpec(first.shape, lambda a: (0, 0, 0)),
            pl.BlockSpec(rest.shape, lambda a: (0, 0, 0)),
            pl.BlockSpec((2, 2, nb, nb // 2), lambda a: (0, 0, a, 0)),
            pl.BlockSpec(top.shape, lambda a: (0, 0, 0, 0, 0)),
        ],
        out_specs=pl.BlockSpec((1, ca, nb, nb), lambda a: (a, 0, 0, 0)),
        out_shape=jax.ShapeDtypeStruct(matrix.shape, BF),
        scratch_shapes=[
            VM((2, ca, nb, nb), BF),
            VM((2, 3, nb, nb), BF),
            VM((2, 2, 2 * nb, nb), BF),
        ],
        compiler_params=pltpu.CompilerParams(vmem_limit_bytes=48 << 20),
        name="update",
    )(at, matrix, first, rest, panel, top)


def body(nr, nx, ny, matrix, pivots):
    r = lax.axis_index("row")
    matrix = matrix.transpose(0, 2, 1, 3)
    nb = matrix.shape[2]
    source, target = interchange(pivots, nb)

    def local(rows, valid):
        index = rows // (nb * nr) * nb + rows % nb
        return jnp.where(jnp.logical_and(valid, rows // nb % nr == r), index, -1)

    where = local(source, True)[:, None]
    at = local(target, target >= 2 * nb)[None, :]
    first, rest, src = pick(matrix, where)
    first, rest, panel, top = exchange(first, rest, src, nr // 2, nx, ny, 1)
    out = update(matrix, at, first, rest, panel, top, nr)
    return out.transpose(0, 2, 1, 3)


def solution(mesh):
    nr, ncol = mesh.shape["row"], mesh.shape["col"]
    ny = int(ncol**0.5)
    return jax.shard_map(
        functools.partial(body, nr, ncol // ny, ny),
        mesh=mesh,
        in_specs=(P(None, "row", None, "col"), P()),
        out_specs=P(None, "row", None, "col"),
        check_vma=False,
    )
```
